32 devices in a mesh: row: 4 (over y, core), col: 8 (over z, x).
Axes of the slice: x: 2, y: 2, z: 4, core: 2. Of those that a mesh axis runs over, the one named last changes fastest.
Arguments:
- left_image: bfloat16 [32, 1024], P('row', 'col'), may hold values from -6 to 6
- right_image: bfloat16 [32, 1024], P('row', 'col'), may hold values from -6 to 6
- first_weight: bfloat16 [32, 9], replicated, may hold values from -2 to 2
- second_weight: bfloat16 [32, 288], replicated, may hold values from -0.375 to 0.375
- third_weight: bfloat16 [32, 288], replicated, may hold values from -0.375 to 0.375
- tile_base: int32 [4, 8], P('row', 'col'), may hold values from 0 to 96, as said below
- tile_width: int32 [4, 8], P('row', 'col'), may hold values from 32 to 128
Outputs:
- aggregated: bfloat16 [32, 1024, 128], P('row', 'col')
The draws below stay inside these ranges and needn't reach their ends.
Inputs may be any that keep to these rules, and one draw needn't show every extreme that they name: In every tile tile_base + tile_width <= 128; one tile has tile_base 0 and tile_width 128, another has tile_base 128 - 128 // 4 and tile_width 128 // 4.
All inputs are finite; a program needn't handle non-finite values.
Results may differ from the reference program's by a relative error of at most 0.0045.
Values may be sent and summed in bfloat16 or wider, within the bound.
A program may use at most 64 MiB of HBM per device.

```python
import jax
import jax.numpy as jnp
from jax import lax

CH = 32
NDISP = 128
TR = 8
TC = 128
HEIGHT = 32
WIDTH = 1024
TILE_ROWS = 4
TILE_COLS = 8


def tile_pair(key):
    inner_key = jax.random.fold_in(key, 7)
    key_width, key_order, key_base = jax.random.split(inner_key, 3)
    count_all = TILE_ROWS * TILE_COLS
    widths = jax.random.randint(key_width, (count_all,), NDISP // 4, NDISP + 1)
    ordering = jax.random.permutation(key_order, count_all)
    widths = widths.at[ordering[0]].set(NDISP).at[ordering[1]].set(NDISP // 4)
    bases = jax.random.randint(key_base, (count_all,), 0, NDISP - widths + 1)
    bases = bases.at[ordering[0]].set(0).at[ordering[1]].set(NDISP - NDISP // 4)
    return (bases.reshape(TILE_ROWS, TILE_COLS).astype(jnp.int32), widths.reshape(TILE_ROWS, TILE_COLS).astype(jnp.int32))


def draw_tile_base(key, part):
    return tile_pair(key)[0]


def draw_tile_width(key, part):
    return tile_pair(key)[1]


def drawn_boxes(key):
    inner_key = jax.random.fold_in(key, 11)
    key_col, key_row = jax.random.split(inner_key)
    box_cols = WIDTH // 4
    box_rows = HEIGHT - HEIGHT // 4
    col_start = jax.random.randint(key_col, (2,), 0, WIDTH - box_cols + 1)
    row_start = jax.random.randint(key_row, (2,), HEIGHT // 16, HEIGHT // 8 + 1)
    return (col_start, row_start, box_cols, box_rows)


def image_with_boxes(key, salt):
    col_start, row_start, box_cols, box_rows = drawn_boxes(key)
    own_key = jax.random.fold_in(key, salt)
    key_tex, key_level = jax.random.split(own_key)
    texture = jnp.clip(jax.random.normal(key_tex, (HEIGHT, WIDTH), jnp.float32), -6.0, 6.0)
    levels = jax.random.uniform(key_level, (2,), jnp.float32, -1.5, 1.5)
    row_place = jnp.arange(HEIGHT)[:, None]
    col_place = jnp.arange(WIDTH)[None, :]
    picture = texture
    for box_num in range(2):
        inside = (row_place >= row_start[box_num]) & (row_place < row_start[box_num] + box_rows) & (col_place >= col_start[box_num]) & (col_place < col_start[box_num] + box_cols)
        picture = jnp.where(inside, levels[box_num], picture)
    return picture.astype(jnp.bfloat16)


def draw_left_image(key, part):
    return image_with_boxes(key, 21)


def draw_right_image(key, part):
    return image_with_boxes(key, 22)


def normal_values(key, extent, deviation, bound, kind=jnp.bfloat16):
    array = deviation * jax.random.normal(key, extent, jnp.float32)
    return jnp.clip(array, min=-bound, max=bound).astype(kind)


def setup_inputs(seed: int = 0) -> dict:
    streams_of = jax.random.split(jax.random.key(seed), 8)
    return {
        "left_image": draw_left_image(jax.random.fold_in(streams_of[7], 71), 0),
        "right_image": draw_right_image(jax.random.fold_in(streams_of[7], 71), 0),
        "first_weight": normal_values(streams_of[2], (CH, 9), 9 ** -0.5, 2.0),
        "second_weight": normal_values(streams_of[3], (CH, 9 * CH), (9 * CH) ** -0.5, 0.375),
        "third_weight": normal_values(streams_of[4], (CH, 9 * CH), (9 * CH) ** -0.5, 0.375),
        "tile_base": draw_tile_base(jax.random.fold_in(streams_of[7], 71), 0),
        "tile_width": draw_tile_width(jax.random.fold_in(streams_of[7], 71), 0),
    }


PENALTY_SMALL = 0.5
PENALTY_LARGE = 4.0
INVALID_COST = 2.0
BIG_VALUE = 1e+30

def conv_layer(current, weight, in_chan, rectify):
    kernel = weight.reshape(CH, 3, 3, in_chan).transpose(0, 3, 1, 2)
    result = lax.conv_general_dilated(current[None], kernel, (1, 1), ((1, 1), (1, 1)), dimension_numbers=('NCHW', 'OIHW', 'NCHW'), preferred_element_type=jnp.float32)[0]
    if rectify:
        result = jnp.maximum(result, 0.0)
    return result.astype(jnp.bfloat16)

def tower(gray_image, first_weight, second_weight, third_weight):
    current = conv_layer(gray_image[None], first_weight, 1, True)
    current = conv_layer(current, second_weight, CH, True)
    return conv_layer(current, third_weight, CH, False)

def feature_norm(features):
    return jnp.maximum(jnp.sqrt(lax.optimization_barrier(jnp.sum(jnp.square(features.astype(jnp.float32)), axis=0))), 1.0)

def path_step(previous, column_cost):
    lowest = lax.optimization_barrier(jnp.min(previous, axis=-1, keepdims=True))
    edge_fill = jnp.full(previous.shape[:-1] + (1,), BIG_VALUE, previous.dtype)
    upper_step = jnp.concatenate([previous[..., 1:], edge_fill], axis=-1)
    lower_step = jnp.concatenate([edge_fill, previous[..., :-1]], axis=-1)
    chosen = jnp.minimum(jnp.minimum(previous, jnp.minimum(upper_step, lower_step) + PENALTY_SMALL), lowest + PENALTY_LARGE)
    updated = column_cost.astype(previous.dtype) + chosen - lowest
    return (updated, updated)

def sweep(volume_major, backward):
    start_state = jnp.zeros(volume_major.shape[1:], jnp.float32)
    final_state, path_costs = lax.scan(path_step, start_state, volume_major, reverse=backward)
    return path_costs

def reference(left_image, right_image, first_weight, second_weight, third_weight, tile_base, tile_width):
    left_feat = tower(left_image, first_weight, second_weight, third_weight)
    right_feat = tower(right_image, first_weight, second_weight, third_weight)
    left_norm = feature_norm(left_feat)
    right_norm = feature_norm(right_feat)
    height_all, width_all = left_image.shape
    right_pad = jnp.concatenate([jnp.zeros((CH, height_all, NDISP), right_feat.dtype), right_feat], axis=2)
    norm_pad = jnp.concatenate([jnp.ones((height_all, NDISP), right_norm.dtype), right_norm], axis=1)
    base_map = jnp.repeat(jnp.repeat(tile_base, TR, axis=0), TC, axis=1)
    width_map = jnp.repeat(jnp.repeat(tile_width, TR, axis=0), TC, axis=1)
    left_wide = left_feat.astype(jnp.float32)

    def one_shift(shift_num):
        offset = (NDISP - shift_num).astype(jnp.int32)
        shifted = lax.dynamic_slice_in_dim(right_pad, offset, width_all, axis=2).astype(jnp.float32)
        shift_norm = lax.dynamic_slice_in_dim(norm_pad, offset, width_all, axis=1)
        cosine = lax.optimization_barrier(jnp.sum(left_wide * shifted, axis=0)) / (left_norm * shift_norm)
        in_range = (shift_num >= base_map) & (shift_num < base_map + width_map)
        return jnp.where(in_range, 1.0 - cosine, INVALID_COST).astype(jnp.bfloat16)
    volume = lax.map(one_shift, jnp.arange(NDISP, dtype=jnp.int32))
    volume = jnp.transpose(volume, (1, 2, 0))
    summed = sweep(volume, False)
    summed = summed + sweep(volume, True)
    columns_first = jnp.swapaxes(volume, 0, 1)
    summed = summed + jnp.swapaxes(sweep(columns_first, False), 0, 1)
    summed = summed + jnp.swapaxes(sweep(columns_first, True), 0, 1)
    return (summed * 0.25).astype(jnp.bfloat16)
```

```python
from functools import partial

import jax
import jax.numpy as jnp
from jax import lax
from jax.experimental import pallas as pl
from jax.experimental.pallas import tpu as pltpu
from jax.sharding import PartitionSpec as P

NDISP = 128
MESH = pl.DeviceIdType.MESH


PENALTY_SMALL = 0.5
PENALTY_LARGE = 4.0
INVALID_COST = 2.0
BIG_VALUE = 1e30


def padded(x, sides, width):
    for axis, dim in sides:
        size, length = (lax.axis_size(axis), x.shape[dim])
        up = [(i, (i + 1) % size) for i in range(size - 1)]
        down = [(j, i) for i, j in up]
        last = lax.slice_in_dim(x, length - width, length, axis=dim)
        initial = lax.slice_in_dim(x, 0, width, axis=dim)
        before = lax.ppermute(last, axis, up)
        after = lax.ppermute(initial, axis, down)
        x = jnp.concatenate([before, x, after], axis=dim)
    return x


def passed_along(value, axis, steps):
    count = lax.axis_size(axis)
    initial, last = (max(0, -steps), min(count, count - steps))
    return lax.ppermute(value, axis, [(source, source + steps) for source in range(initial, last)])


def conv_valid(source, weight):
    in_chan, ext_rows, ext_cols = source.shape
    out_rows = ext_rows - 2
    out_cols = ext_cols - 2
    pieces = [
        source[:, row_off : row_off + out_rows, col_off : col_off + out_cols]
        for row_off in range(3)
        for col_off in range(3)
    ]
    patches = jnp.stack(pieces, 0).reshape(9 * in_chan, out_rows * out_cols)
    result = jnp.dot(weight, patches, preferred_element_type=jnp.float32)
    return result.reshape(weight.shape[0], out_rows, out_cols)


def tower_valid(source, weights, first_row, first_col, total_rows, total_cols):
    current = source[None]
    for layer_num in range(3):
        result = conv_valid(current, weights[layer_num])
        if layer_num < 2:
            result = jnp.maximum(result, 0.0)
        row_place = first_row + layer_num + 1 + jnp.arange(result.shape[1])
        col_place = first_col + layer_num + 1 + jnp.arange(result.shape[2])
        inside = ((row_place >= 0) & (row_place < total_rows))[:, None] & (
            (col_place >= 0) & (col_place < total_cols)
        )[None, :]
        current = jnp.where(inside[None], result, 0.0).astype(jnp.bfloat16)
    return current


def feature_norm(features):
    return jnp.maximum(jnp.sqrt(jnp.sum(jnp.square(features.astype(jnp.float32)), axis=0)), 1.0)


def correlate(left_feat, right_ext, base_disp, range_width):
    chans, tile_rows, tile_cols = left_feat.shape
    left_norm = feature_norm(left_feat)
    right_norm = feature_norm(right_ext)
    products = jnp.einsum("cyx,cyz->yxz", left_feat, right_ext, preferred_element_type=jnp.float32)
    cosine = products / (left_norm[:, :, None] * right_norm[:, None, :])
    ext_span = 2 * tile_cols
    flattened = cosine.reshape(tile_rows, tile_cols * ext_span)
    flattened = jnp.pad(flattened, ((0, 0), (0, tile_cols)))
    skewed = flattened.reshape(tile_rows, tile_cols, ext_span + 1)
    diagonal_band = skewed[:, :, tile_cols - NDISP + 1 : tile_cols + 1][:, :, ::-1]
    shifts = jnp.arange(NDISP)
    in_range = (shifts >= base_disp) & (shifts < base_disp + range_width)
    return jnp.where(in_range, 1.0 - diagonal_band, INVALID_COST).astype(jnp.bfloat16)


def mesh_barrier(col, cols, row, rows):
    barrier = pltpu.get_barrier_semaphore()
    count = jnp.int32(0)
    for axis, place, size in (("col", col, cols), ("row", row, rows)):
        for step in (-1, 1):
            there = (place + step >= 0) & (place + step < size)

            @pl.when(there)
            def _():
                pl.semaphore_signal(
                    barrier, inc=1, device_id={axis: place + step}, device_id_type=MESH
                )

            count = count + there.astype(jnp.int32)
    return barrier, count


def path_kernel(
    tile_rows,
    tile_cols,
    volume_ref,
    out_ref,
    cost,
    acc,
    h_send,
    h_recv,
    v_send,
    v_recv,
    h_send_sem,
    h_recv_sem,
    v_send_sem,
    v_recv_sem,
):
    cols, rows = lax.axis_size("col"), lax.axis_size("row")
    col, row = lax.axis_index("col"), lax.axis_index("row")
    barrier, count = mesh_barrier(col, cols, row, rows)
    cost[...] = volume_ref[...].astype(jnp.float32)
    acc[...] = jnp.zeros_like(acc)
    pl.semaphore_wait(barrier, count)

    def edges(shape):
        lane = lax.broadcasted_iota(jnp.int32, shape, 1)
        low_edge = jnp.where(lane == 0, BIG_VALUE, PENALTY_SMALL)
        high_edge = jnp.where(lane == NDISP - 1, BIG_VALUE, PENALTY_SMALL)
        return low_edge, high_edge

    def near(state, low_edge, high_edge):
        return jnp.minimum(
            state,
            jnp.minimum(
                pltpu.roll(state, 1, 1) + low_edge, pltpu.roll(state, NDISP - 1, 1) + high_edge
            ),
        )

    def run(axis, place, size, backward, send, recv, send_sem, recv_sem, sweep):
        way = backward.astype(jnp.int32)
        step = 1 - 2 * way
        has_source = (place - step >= 0) & (place - step < size)
        has_target = (place + step >= 0) & (place + step < size)
        copy = pltpu.make_async_remote_copy(
            src_ref=send.at[way],
            dst_ref=recv.at[way],
            send_sem=send_sem.at[way],
            recv_sem=recv_sem.at[way],
            device_id={axis: place + step},
            device_id_type=MESH,
        )

        @pl.when(has_source)
        def _():
            copy.wait_recv()

        @pl.when(jnp.logical_not(has_source))
        def _():
            recv[way] = jnp.zeros(recv.shape[1:], jnp.float32)

        send[way] = sweep(recv[way], backward)

        @pl.when(has_target)
        def _():
            copy.start()

        return copy, has_target

    def row_sweep(state, backward):
        low_edge, high_edge = edges(state.shape)

        def body(index, state):
            place = jnp.where(backward, tile_cols - 1 - index, index)
            where = pl.ds(place, tile_rows, stride=tile_cols)
            here = cost[where, :]
            lowest = jnp.min(state, axis=1, keepdims=True)
            updated = jnp.minimum(
                near(state, low_edge, high_edge) + here, lowest + (here + PENALTY_LARGE)
            )
            acc[where, :] = acc[where, :] + (updated - lowest)
            return updated

        state = lax.fori_loop(0, tile_cols, body, state, unroll=4)
        return state - jnp.min(state, axis=1, keepdims=True)

    def column_sweep(state, backward):
        low_edge, high_edge = edges((8, NDISP))

        def body(index, carried):
            place = jnp.where(backward, tile_rows - 1 - index, index)
            new = []
            for piece, state in enumerate(carried):
                where = pl.ds(pl.multiple_of(place * tile_cols + piece * 8, 8), 8)
                lowest = jnp.min(state, axis=1, keepdims=True)
                updated = (
                    jnp.minimum(near(state, low_edge, high_edge), lowest + PENALTY_LARGE)
                    - lowest
                    + cost[where, :]
                )
                acc[where, :] = acc[where, :] + updated
                new.append(updated)
            return tuple(new)

        pieces = tuple(state[i * 8 : i * 8 + 8] for i in range(tile_cols // 8))
        return jnp.concatenate(lax.fori_loop(0, tile_rows, body, pieces), axis=0)

    def horizontal(turn):
        right_half = col > cols - 1 - col
        backward = right_half if turn == 0 else jnp.logical_not(right_half)
        return run(
            "col", col, cols, backward, h_send, h_recv, h_send_sem, h_recv_sem, row_sweep
        )

    def vertical():
        def one(turn, carried):
            lower_half = row > rows - 1 - row
            backward = lower_half != (turn == 1)
            copy, sent = run(
                "row", row, rows, backward, v_send, v_recv, v_send_sem, v_recv_sem, column_sweep
            )

            @pl.when(sent)
            def _():
                copy.wait_send()

            return carried

        lax.fori_loop(0, 2, one, 0)

    late = 2 * jnp.minimum(col, cols - 1 - col) >= cols // 2

    @pl.when(late)
    def _():
        vertical()

    first, first_sent = horizontal(0)

    @pl.when(jnp.logical_not(late))
    def _():
        vertical()

    second, second_sent = horizontal(1)
    out_ref[...] = (acc[...] * 0.25).astype(jnp.bfloat16)

    @pl.when(first_sent)
    def _():
        first.wait_send()

    @pl.when(second_sent)
    def _():
        second.wait_send()


def aggregate(volume):
    tile_rows, tile_cols, disps = volume.shape
    count = tile_rows * tile_cols
    out = pl.pallas_call(
        partial(path_kernel, tile_rows, tile_cols),
        out_shape=jax.ShapeDtypeStruct((count, disps), jnp.bfloat16),
        in_specs=[pl.BlockSpec(memory_space=pltpu.VMEM)],
        out_specs=pl.BlockSpec(memory_space=pltpu.VMEM),
        scratch_shapes=[
            pltpu.VMEM((count, disps), jnp.float32),
            pltpu.VMEM((count, disps), jnp.float32),
            pltpu.VMEM((2, tile_rows, disps), jnp.float32),
            pltpu.VMEM((2, tile_rows, disps), jnp.float32),
            pltpu.VMEM((2, tile_cols, disps), jnp.float32),
            pltpu.VMEM((2, tile_cols, disps), jnp.float32),
            pltpu.SemaphoreType.DMA((2,)),
            pltpu.SemaphoreType.DMA((2,)),
            pltpu.SemaphoreType.DMA((2,)),
            pltpu.SemaphoreType.DMA((2,)),
        ],
        compiler_params=pltpu.CompilerParams(collective_id=0, has_side_effects=True),
        name="paths",
    )(volume.reshape(count, disps))
    return out.reshape(tile_rows, tile_cols, disps)


def on_device(
    left_image, right_image, first_weight, second_weight, third_weight, tile_base, tile_width
):
    weights = (first_weight, second_weight, third_weight)
    tile_rows, tile_cols = left_image.shape
    margins = padded(jnp.stack([left_image, right_image]), (("row", 1), ("col", 2)), 3)
    total_rows = tile_rows * lax.axis_size("row")
    total_cols = tile_cols * lax.axis_size("col")
    first_row = lax.axis_index("row") * tile_rows - 3
    first_col = lax.axis_index("col") * tile_cols - 3
    left_feat = tower_valid(margins[0], weights, first_row, first_col, total_rows, total_cols)
    neighbour = passed_along(margins[1], "col", 1)
    joined = jnp.concatenate([neighbour[:, :tile_cols], margins[1]], axis=1)
    right_ext = tower_valid(
        joined, weights, first_row, first_col - tile_cols, total_rows, total_cols
    )
    volume = correlate(left_feat, right_ext, tile_base[0, 0], tile_width[0, 0])
    return aggregate(volume)


def solution(mesh):
    placed = (P("row", "col"), P("row", "col"), P(), P(), P(), P("row", "col"), P("row", "col"))
    return jax.shard_map(
        on_device, mesh=mesh, in_specs=placed, out_specs=P("row", "col", None), check_vma=False
    )
```

```python
from functools import partial

import jax
import jax.numpy as jnp
from jax import lax
from jax.experimental import pallas as pl
from jax.experimental.pallas import tpu as pltpu
from jax.sharding import PartitionSpec as P

NDISP = 128
MESH = pl.DeviceIdType.MESH


PENALTY_SMALL = 0.5
PENALTY_LARGE = 4.0
INVALID_COST = 2.0
BIG_VALUE = 1e30


def padded(x, sides, width):
    for axis, dim in sides:
        size, length = (lax.axis_size(axis), x.shape[dim])
        up = [(i, (i + 1) % size) for i in range(size - 1)]
        down = [(j, i) for i, j in up]
        last = lax.slice_in_dim(x, length - width, length, axis=dim)
        initial = lax.slice_in_dim(x, 0, width, axis=dim)
        before = lax.ppermute(last, axis, up)
        after = lax.ppermute(initial, axis, down)
        x = jnp.concatenate([before, x, after], axis=dim)
    return x


def passed_along(value, axis, steps):
    count = lax.axis_size(axis)
    initial, last = (max(0, -steps), min(count, count - steps))
    return lax.ppermute(value, axis, [(source, source + steps) for source in range(initial, last)])


def conv_valid(source, weight):
    in_chan, ext_rows, ext_cols = source.shape
    out_rows = ext_rows - 2
    out_cols = ext_cols - 2
    pieces = [
        source[:, row_off : row_off + out_rows, col_off : col_off + out_cols]
        for row_off in range(3)
        for col_off in range(3)
    ]
    patches = jnp.stack(pieces, 0).reshape(9 * in_chan, out_rows * out_cols)
    result = jnp.dot(weight, patches, preferred_element_type=jnp.float32)
    return result.reshape(weight.shape[0], out_rows, out_cols)


def tower_valid(source, weights, first_row, first_col, total_rows, total_cols):
    current = source[None]
    for layer_num in range(3):
        result = conv_valid(current, weights[layer_num])
        if layer_num < 2:
            result = jnp.maximum(result, 0.0)
        row_place = first_row + layer_num + 1 + jnp.arange(result.shape[1])
        col_place = first_col + layer_num + 1 + jnp.arange(result.shape[2])
        inside = ((row_place >= 0) & (row_place < total_rows))[:, None] & (
            (col_place >= 0) & (col_place < total_cols)
        )[None, :]
        current = jnp.where(inside[None], result, 0.0).astype(jnp.bfloat16)
    return current


def feature_norm(features):
    return jnp.maximum(jnp.sqrt(jnp.sum(jnp.square(features.astype(jnp.float32)), axis=0)), 1.0)


def correlate(left_feat, right_ext, base_disp, range_width):
    chans, tile_rows, tile_cols = left_feat.shape
    left_norm = feature_norm(left_feat)
    right_norm = feature_norm(right_ext)
    products = jnp.einsum("cyx,cyz->yxz", left_feat, right_ext, preferred_element_type=jnp.float32)
    cosine = products / (left_norm[:, :, None] * right_norm[:, None, :])
    ext_span = 2 * tile_cols
    flattened = cosine.reshape(tile_rows, tile_cols * ext_span)
    flattened = jnp.pad(flattened, ((0, 0), (0, tile_cols)))
    skewed = flattened.reshape(tile_rows, tile_cols, ext_span + 1)
    diagonal_band = skewed[:, :, tile_cols - NDISP + 1 : tile_cols + 1][:, :, ::-1]
    shifts = jnp.arange(NDISP)
    in_range = (shifts >= base_disp) & (shifts < base_disp + range_width)
    return jnp.where(in_range, 1.0 - diagonal_band, INVALID_COST).astype(jnp.bfloat16)


def mesh_barrier(col, cols, row, rows):
    barrier = pltpu.get_barrier_semaphore()
    count = jnp.int32(0)
    for axis, place, size in (("col", col, cols), ("row", row, rows)):
        for step in (-1, 1):
            there = (place + step >= 0) & (place + step < size)

            @pl.when(there)
            def _():
                pl.semaphore_signal(
                    barrier, inc=1, device_id={axis: place + step}, device_id_type=MESH
                )

            count = count + there.astype(jnp.int32)
    return barrier, count


SUBS = 8
LEADS = NDISP // SUBS


def path_kernel(
    tile_rows,
    tile_cols,
    volume_ref,
    out_ref,
    v_cost,
    h_cost,
    h_path,
    v_path,
    total,
    h_send,
    h_recv,
    v_send,
    v_recv,
    h_send_sem,
    h_recv_sem,
    v_send_sem,
    v_recv_sem,
):
    cols, rows = lax.axis_size("col"), lax.axis_size("row")
    col, row = lax.axis_index("col"), lax.axis_index("row")
    barrier, count = mesh_barrier(col, cols, row, rows)
    span = NDISP // tile_rows
    groups = tile_cols // span
    vreg = (SUBS, NDISP)
    sub = lax.broadcasted_iota(jnp.int32, vreg, 0)
    lane = lax.broadcasted_iota(jnp.int32, vreg, 1)
    first_edge = jnp.where(sub == 0, BIG_VALUE, 0.0)
    last_edge = jnp.where(sub == SUBS - 1, BIG_VALUE, 0.0)
    near_row = lax.broadcasted_iota(jnp.int32, (NDISP, NDISP), 0)
    near_col = lax.broadcasted_iota(jnp.int32, (NDISP, NDISP), 1)
    order = ((near_row % SUBS) * LEADS + near_row // SUBS == near_col).astype(jnp.float32)
    order = order.astype(jnp.bfloat16)

    def ordered(block):
        return lax.dot_general(
            order, block, (((1,), (1,)), ((), ())), preferred_element_type=jnp.float32
        )

    def restored(block):
        turned = block.T
        high = turned.astype(jnp.bfloat16)
        low = (turned - high.astype(jnp.float32)).astype(jnp.bfloat16)
        return jnp.dot(high, order, preferred_element_type=jnp.float32) + jnp.dot(
            low, order, preferred_element_type=jnp.float32
        )

    def spread(group, carried):
        start = pl.multiple_of(group * span, span)
        block = jnp.concatenate(
            [volume_ref[y, pl.ds(start, span), :] for y in range(tile_rows)], axis=0
        )
        block = ordered(block)
        for lead in range(LEADS):
            piece = block[lead * SUBS : lead * SUBS + SUBS]
            for x in range(span):
                h_cost[start + x, lead] = pltpu.roll(piece, (NDISP - x) % NDISP, 1)
        return carried

    lax.fori_loop(0, groups, spread, 0)
    pl.semaphore_wait(barrier, count)

    def advance(state, here):
        lowest = list(state)
        while len(lowest) > 1:
            lowest = [jnp.minimum(lowest[i], lowest[i + 1]) for i in range(0, len(lowest), 2)]
        lowest = lowest[0]
        for shift in (4, 2, 1):
            lowest = jnp.minimum(lowest, pltpu.roll(lowest, shift, 0))
        below = jnp.maximum(pltpu.roll(state[LEADS - 1], 1, 0), first_edge)
        above = jnp.maximum(pltpu.roll(state[0], SUBS - 1, 0), last_edge)
        ext = [below, *state, above]
        new = []
        for lead in range(LEADS):
            near = jnp.minimum(
                state[lead], jnp.minimum(ext[lead], ext[lead + 2]) + PENALTY_SMALL
            )
            new.append(
                jnp.minimum(near + here[lead], lowest + (here[lead] + PENALTY_LARGE))
            )
        return tuple(new), lowest

    def run(axis, place, size, backward, send, recv, send_sem, recv_sem, sweep):
        way = backward.astype(jnp.int32)
        step = 1 - 2 * way
        has_source = (place - step >= 0) & (place - step < size)
        has_target = (place + step >= 0) & (place + step < size)
        copy = pltpu.make_async_remote_copy(
            src_ref=send.at[way],
            dst_ref=recv.at[way],
            send_sem=send_sem.at[way],
            recv_sem=recv_sem.at[way],
            device_id={axis: place + step},
            device_id_type=MESH,
        )

        @pl.when(has_source)
        def _():
            copy.wait_recv()

        @pl.when(jnp.logical_not(has_source))
        def _():
            recv[way] = jnp.zeros(recv.shape[1:], jnp.float32)

        sweep(way, backward)

        @pl.when(has_target)
        def _():
            copy.start()

        return copy, has_target

    def row_sweep(way, backward):
        packed = h_recv[way]
        state = tuple(pltpu.roll(packed, (NDISP - i) % NDISP, 1) for i in range(LEADS))

        def body(index, carried):
            place = jnp.where(backward, tile_cols - 1 - index, index)
            here = [h_cost[place, lead] for lead in range(LEADS)]
            state, lowest = advance(carried[0], here)
            for lead in range(LEADS):
                h_path[way, place, lead] = state[lead] - lowest
            return state, lowest

        state, lowest = lax.fori_loop(
            0, tile_cols, body, (state, jnp.zeros(vreg, jnp.float32)), unroll=2
        )
        packed = state[0] - lowest
        for lead in range(1, LEADS):
            moved = pltpu.roll(state[lead] - lowest, lead, 1)
            packed = jnp.where(lane % span == lead, moved, packed)
        h_send[way] = packed

    def column_sweep(way, backward):
        state = tuple(v_recv[way, lead] for lead in range(LEADS))

        def body(index, state):
            place = jnp.where(backward, tile_rows - 1 - index, index)
            here = [v_cost[place, lead] for lead in range(LEADS)]
            state, lowest = advance(state, here)
            for lead in range(LEADS):
                v_path[way, place, lead] = state[lead] - lowest
            return tuple(value - lowest for value in state)

        state = lax.fori_loop(0, tile_rows, body, state)
        for lead in range(LEADS):
            v_send[way, lead] = state[lead]

    def horizontal(turn):
        right_half = col > cols - 1 - col
        backward = right_half if turn == 0 else jnp.logical_not(right_half)
        return run(
            "col", col, cols, backward, h_send, h_recv, h_send_sem, h_recv_sem, row_sweep
        )

    def vertical():
        def place_row(y, carried):
            block = ordered(volume_ref[y])
            for lead in range(LEADS):
                v_cost[y, lead] = block[lead * SUBS : lead * SUBS + SUBS]
            return carried

        lax.fori_loop(0, tile_rows, place_row, 0)

        def one(turn, carried):
            lower_half = row > rows - 1 - row
            backward = lower_half != (turn == 1)
            copy, sent = run(
                "row", row, rows, backward, v_send, v_recv, v_send_sem, v_recv_sem, column_sweep
            )

            @pl.when(sent)
            def _():
                copy.wait_send()

            return carried

        lax.fori_loop(0, 2, one, 0)

        def gather_row(y, carried):
            block = jnp.concatenate(
                [v_path[0, y, lead] + v_path[1, y, lead] for lead in range(LEADS)], axis=0
            )
            total[y] = restored(block)
            return carried

        lax.fori_loop(0, tile_rows, gather_row, 0)

    late = 2 * jnp.minimum(col, cols - 1 - col) >= cols // 2

    @pl.when(late)
    def _():
        vertical()

    first, first_sent = horizontal(0)

    @pl.when(jnp.logical_not(late))
    def _():
        vertical()

    second, second_sent = horizontal(1)

    def gather(group, carried):
        start = pl.multiple_of(group * span, span)
        pieces = []
        for lead in range(LEADS):
            merged = h_path[0, start, lead] + h_path[1, start, lead]
            for x in range(1, span):
                moved = pltpu.roll(h_path[0, start + x, lead] + h_path[1, start + x, lead], x, 1)
                merged = jnp.where(lane % span == x, moved, merged)
            pieces.append(merged)
        block = restored(jnp.concatenate(pieces, axis=0))
        for y in range(tile_rows):
            where = pl.ds(start, span)
            out_ref[y, where, :] = (
                (total[y, where, :] + block[y * span : y * span + span]) * 0.25
            ).astype(jnp.bfloat16)
        return carried

    lax.fori_loop(0, groups, gather, 0)

    @pl.when(first_sent)
    def _():
        first.wait_send()

    @pl.when(second_sent)
    def _():
        second.wait_send()


def aggregate(volume):
    tile_rows, tile_cols, disps = volume.shape
    vregs = (LEADS, SUBS, NDISP)
    return pl.pallas_call(
        partial(path_kernel, tile_rows, tile_cols),
        out_shape=jax.ShapeDtypeStruct(volume.shape, jnp.bfloat16),
        in_specs=[pl.BlockSpec(memory_space=pltpu.VMEM)],
        out_specs=pl.BlockSpec(memory_space=pltpu.VMEM),
        scratch_shapes=[
            pltpu.VMEM((tile_rows, *vregs), jnp.float32),
            pltpu.VMEM((tile_cols, *vregs), jnp.float32),
            pltpu.VMEM((2, tile_cols, *vregs), jnp.float32),
            pltpu.VMEM((2, tile_rows, *vregs), jnp.float32),
            pltpu.VMEM(volume.shape, jnp.float32),
            pltpu.VMEM((2, SUBS, NDISP), jnp.float32),
            pltpu.VMEM((2, SUBS, NDISP), jnp.float32),
            pltpu.VMEM((2, *vregs), jnp.float32),
            pltpu.VMEM((2, *vregs), jnp.float32),
            pltpu.SemaphoreType.DMA((2,)),
            pltpu.SemaphoreType.DMA((2,)),
            pltpu.SemaphoreType.DMA((2,)),
            pltpu.SemaphoreType.DMA((2,)),
        ],
        compiler_params=pltpu.CompilerParams(
            collective_id=0, has_side_effects=True, vmem_limit_bytes=48 << 20
        ),
        name="paths",
    )(volume)


def on_device(
    left_image, right_image, first_weight, second_weight, third_weight, tile_base, tile_width
):
    weights = (first_weight, second_weight, third_weight)
    tile_rows, tile_cols = left_image.shape
    margins = padded(jnp.stack([left_image, right_image]), (("row", 1), ("col", 2)), 3)
    total_rows = tile_rows * lax.axis_size("row")
    total_cols = tile_cols * lax.axis_size("col")
    first_row = lax.axis_index("row") * tile_rows - 3
    first_col = lax.axis_index("col") * tile_cols - 3
    left_feat = tower_valid(margins[0], weights, first_row, first_col, total_rows, total_cols)
    neighbour = passed_along(margins[1], "col", 1)
    joined = jnp.concatenate([neighbour[:, :tile_cols], margins[1]], axis=1)
    right_ext = tower_valid(
        joined, weights, first_row, first_col - tile_cols, total_rows, total_cols
    )
    volume = correlate(left_feat, right_ext, tile_base[0, 0], tile_width[0, 0])
    return aggregate(volume)


def solution(mesh):
    placed = (P("row", "col"), P("row", "col"), P(), P(), P(), P("row", "col"), P("row", "col"))
    return jax.shard_map(
        on_device, mesh=mesh, in_specs=placed, out_specs=P("row", "col", None), check_vma=False
    )
```

```python
from functools import partial

import jax
import jax.numpy as jnp
from jax import lax
from jax.experimental import pallas as pl
from jax.experimental.pallas import tpu as pltpu
from jax.sharding import PartitionSpec as P

NDISP = 128
MESH = pl.DeviceIdType.MESH


PENALTY_SMALL = 0.5
PENALTY_LARGE = 4.0
INVALID_COST = 2.0
BIG_VALUE = 1e30


ROW_BLOCKS = 3
COL_BLOCKS = 4


def exchange_kernel(own_ref, out_ref, send_sem, recv_sem):
    cols, rows = lax.axis_size("col"), lax.axis_size("row")
    col, row = lax.axis_index("col"), lax.axis_index("row")
    barrier = pltpu.get_barrier_semaphore()
    moves = [
        (down, right)
        for down in (-1, 0, 1)
        for right in (-1, 0, 1, 2)
        if (down, right) != (0, 0)
    ]

    def exists(down, right):
        return (
            (row + down >= 0) & (row + down < rows) & (col + right >= 0) & (col + right < cols)
        )

    count = jnp.int32(0)
    for down, right in moves:

        @pl.when(exists(-down, -right))
        def _():
            pl.semaphore_signal(
                barrier,
                inc=1,
                device_id={"row": row - down, "col": col - right},
                device_id_type=MESH,
            )

        count = count + exists(down, right).astype(jnp.int32)
    out_ref[1, 2] = own_ref[...]
    pl.semaphore_wait(barrier, count)

    def copy_of(down, right):
        return pltpu.make_async_remote_copy(
            src_ref=own_ref,
            dst_ref=out_ref.at[1 - down, 2 - right],
            send_sem=send_sem.at[1 - down, 2 - right],
            recv_sem=recv_sem.at[1 - down, 2 - right],
            device_id={"row": row + down, "col": col + right},
            device_id_type=MESH,
        )

    for down, right in moves:

        @pl.when(exists(down, right))
        def _():
            copy_of(down, right).start()

        @pl.when(jnp.logical_not(exists(-down, -right)))
        def _():
            out_ref[1 - down, 2 - right] = jnp.zeros(own_ref.shape, jnp.float32)

    for down, right in moves:

        @pl.when(exists(-down, -right))
        def _():
            copy_of(down, right).wait_recv()

        @pl.when(exists(down, right))
        def _():
            copy_of(down, right).wait_send()


def exchange(images):
    shape = (ROW_BLOCKS, COL_BLOCKS, *images.shape)
    return pl.pallas_call(
        exchange_kernel,
        out_shape=jax.ShapeDtypeStruct(shape, jnp.float32),
        in_specs=[pl.BlockSpec(memory_space=pltpu.VMEM)],
        out_specs=pl.BlockSpec(memory_space=pltpu.VMEM),
        scratch_shapes=[
            pltpu.SemaphoreType.DMA((ROW_BLOCKS, COL_BLOCKS)),
            pltpu.SemaphoreType.DMA((ROW_BLOCKS, COL_BLOCKS)),
        ],
        compiler_params=pltpu.CompilerParams(collective_id=1, has_side_effects=True),
        name="exchange",
    )(images)


def layer(source, weight, span, out_rows, rectify, inside):
    chans, length = source.shape
    stacked = jnp.concatenate(
        [pltpu.roll(source, 1, 1), source, pltpu.roll(source, length - 1, 1)], axis=0
    ).astype(jnp.bfloat16)
    result = jnp.zeros((weight.shape[0], out_rows * span), jnp.float32)
    for row_off in range(3):
        result = result + jnp.dot(
            weight[:, row_off * 3 * chans : (row_off + 1) * 3 * chans],
            stacked[:, row_off * span : (row_off + out_rows) * span],
            preferred_element_type=jnp.float32,
        )
    if rectify:
        result = jnp.maximum(result, 0.0)
    return jnp.where(inside, result, 0.0).astype(jnp.bfloat16).astype(jnp.float32)


def cost_kernel(
    tile_rows, tile_cols, place_ref, blocks_ref, first_ref, second_ref, third_ref, out_ref
):
    base, width = place_ref[0], place_ref[1]
    first_row, first_col = place_ref[2], place_ref[3]
    total_rows, total_cols = place_ref[4], place_ref[5]
    weights = (first_ref[...], second_ref[...], third_ref[...])

    def tower(image, blocks):
        span = len(blocks) * tile_cols
        lines = [
            jnp.concatenate([blocks_ref[0, j, image] for j in blocks], axis=1)[
                tile_rows - 3 : tile_rows
            ],
            jnp.concatenate([blocks_ref[1, j, image] for j in blocks], axis=1),
            jnp.concatenate([blocks_ref[2, j, image] for j in blocks], axis=1)[0:3],
        ]
        current = jnp.concatenate(
            [line[i : i + 1] for line in lines for i in range(line.shape[0])], axis=1
        )
        for num in range(3):
            out_rows = tile_rows + 4 - 2 * num
            index = lax.broadcasted_iota(jnp.int32, (1, out_rows * span), 1)
            row_place = first_row - 2 + num + index // span
            col_place = first_col + (blocks[0] - 2) * tile_cols + index % span
            inside = (
                (row_place >= 0)
                & (row_place < total_rows)
                & (col_place >= 0)
                & (col_place < total_cols)
            )
            current = layer(current, weights[num], span, out_rows, num < 2, inside)
        return current, span

    left, left_span = tower(0, (1, 2, 3))
    right, right_span = tower(1, (0, 1, 2, 3))
    ext = 2 * tile_cols
    flip = lax.broadcasted_iota(jnp.int32, (ext, ext), 0) + lax.broadcasted_iota(
        jnp.int32, (ext, ext), 1
    )
    flip = (flip == ext - 1).astype(jnp.float32).astype(jnp.bfloat16)
    shifts = lax.broadcasted_iota(jnp.int32, (tile_cols, NDISP), 1)
    in_range = (shifts >= base) & (shifts < base + width)
    for y in range(tile_rows):
        own = left[:, y * left_span + tile_cols : y * left_span + 2 * tile_cols].T
        other = right[:, y * right_span + tile_cols : y * right_span + 3 * tile_cols]
        other = jnp.dot(other.astype(jnp.bfloat16), flip, preferred_element_type=jnp.float32)
        own_norm = jnp.maximum(jnp.sqrt(jnp.sum(own * own, axis=1, keepdims=True)), 1.0)
        other_norm = jnp.maximum(jnp.sqrt(jnp.sum(other * other, axis=0, keepdims=True)), 1.0)
        products = jnp.dot(
            own.astype(jnp.bfloat16),
            other.astype(jnp.bfloat16),
            preferred_element_type=jnp.float32,
        )
        cosine = products / (own_norm * other_norm)
        cosine = pltpu.roll(cosine, ext - tile_cols + 1, 1, stride=1, stride_axis=0)
        out_ref[y] = jnp.where(in_range, 1.0 - cosine[:, :NDISP], INVALID_COST).astype(
            jnp.bfloat16
        )


def cost_volume(place, blocks, weights):
    tile_rows, tile_cols = blocks.shape[3:]
    return pl.pallas_call(
        partial(cost_kernel, tile_rows, tile_cols),
        out_shape=jax.ShapeDtypeStruct((tile_rows, tile_cols, NDISP), jnp.bfloat16),
        in_specs=[pl.BlockSpec(memory_space=pltpu.SMEM)]
        + [pl.BlockSpec(memory_space=pltpu.VMEM)] * 4,
        out_specs=pl.BlockSpec(memory_space=pltpu.VMEM),
        compiler_params=pltpu.CompilerParams(vmem_limit_bytes=32 << 20),
        name="costs",
    )(place, blocks, *weights)


def mesh_barrier(col, cols, row, rows):
    barrier = pltpu.get_barrier_semaphore()
    count = jnp.int32(0)
    for axis, place, size in (("col", col, cols), ("row", row, rows)):
        for step in (-1, 1):
            there = (place + step >= 0) & (place + step < size)

            @pl.when(there)
            def _():
                pl.semaphore_signal(
                    barrier, inc=1, device_id={axis: place + step}, device_id_type=MESH
                )

            count = count + there.astype(jnp.int32)
    return barrier, count


SUBS = 8
LEADS = NDISP // SUBS


def path_kernel(
    tile_rows,
    tile_cols,
    volume_ref,
    out_ref,
    v_cost,
    h_cost,
    h_path,
    v_path,
    total,
    h_send,
    h_recv,
    v_send,
    v_recv,
    h_send_sem,
    h_recv_sem,
    v_send_sem,
    v_recv_sem,
):
    cols, rows = lax.axis_size("col"), lax.axis_size("row")
    col, row = lax.axis_index("col"), lax.axis_index("row")
    barrier, count = mesh_barrier(col, cols, row, rows)
    span = NDISP // tile_rows
    groups = tile_cols // span
    vreg = (SUBS, NDISP)
    sub = lax.broadcasted_iota(jnp.int32, vreg, 0)
    lane = lax.broadcasted_iota(jnp.int32, vreg, 1)
    first_edge = jnp.where(sub == 0, BIG_VALUE, 0.0)
    last_edge = jnp.where(sub == SUBS - 1, BIG_VALUE, 0.0)
    near_row = lax.broadcasted_iota(jnp.int32, (NDISP, NDISP), 0)
    near_col = lax.broadcasted_iota(jnp.int32, (NDISP, NDISP), 1)
    order = ((near_row % SUBS) * LEADS + near_row // SUBS == near_col).astype(jnp.float32)
    order = order.astype(jnp.bfloat16)

    def ordered(block):
        return lax.dot_general(
            order, block, (((1,), (1,)), ((), ())), preferred_element_type=jnp.float32
        )

    def restored(block):
        turned = block.T
        high = turned.astype(jnp.bfloat16)
        low = (turned - high.astype(jnp.float32)).astype(jnp.bfloat16)
        return jnp.dot(high, order, preferred_element_type=jnp.float32) + jnp.dot(
            low, order, preferred_element_type=jnp.float32
        )

    def spread(group, carried):
        start = pl.multiple_of(group * span, span)
        block = jnp.concatenate(
            [volume_ref[y, pl.ds(start, span), :] for y in range(tile_rows)], axis=0
        )
        block = ordered(block)
        for lead in range(LEADS):
            piece = block[lead * SUBS : lead * SUBS + SUBS]
            for x in range(span):
                h_cost[start + x, lead] = pltpu.roll(piece, (NDISP - x) % NDISP, 1)
        return carried

    lax.fori_loop(0, groups, spread, 0)
    pl.semaphore_wait(barrier, count)

    def advance(state, here):
        lowest = list(state)
        while len(lowest) > 1:
            lowest = [jnp.minimum(lowest[i], lowest[i + 1]) for i in range(0, len(lowest), 2)]
        lowest = lowest[0]
        for shift in (4, 2, 1):
            lowest = jnp.minimum(lowest, pltpu.roll(lowest, shift, 0))
        below = jnp.maximum(pltpu.roll(state[LEADS - 1], 1, 0), first_edge)
        above = jnp.maximum(pltpu.roll(state[0], SUBS - 1, 0), last_edge)
        ext = [below, *state, above]
        new = []
        for lead in range(LEADS):
            near = jnp.minimum(
                state[lead], jnp.minimum(ext[lead], ext[lead + 2]) + PENALTY_SMALL
            )
            new.append(
                jnp.minimum(near + here[lead], lowest + (here[lead] + PENALTY_LARGE))
            )
        return tuple(new), lowest

    def run(axis, place, size, backward, send, recv, send_sem, recv_sem, sweep):
        way = backward.astype(jnp.int32)
        step = 1 - 2 * way
        has_source = (place - step >= 0) & (place - step < size)
        has_target = (place + step >= 0) & (place + step < size)
        copy = pltpu.make_async_remote_copy(
            src_ref=send.at[way],
            dst_ref=recv.at[way],
            send_sem=send_sem.at[way],
            recv_sem=recv_sem.at[way],
            device_id={axis: place + step},
            device_id_type=MESH,
        )

        @pl.when(has_source)
        def _():
            copy.wait_recv()

        @pl.when(jnp.logical_not(has_source))
        def _():
            recv[way] = jnp.zeros(recv.shape[1:], jnp.float32)

        sweep(way, backward)

        @pl.when(has_target)
        def _():
            copy.start()

        return copy, has_target

    def row_sweep(way, backward):
        packed = h_recv[way]
        state = tuple(pltpu.roll(packed, (NDISP - i) % NDISP, 1) for i in range(LEADS))

        def body(index, carried):
            place = jnp.where(backward, tile_cols - 1 - index, index)
            here = [h_cost[place, lead] for lead in range(LEADS)]
            state, lowest = advance(carried[0], here)
            for lead in range(LEADS):
                h_path[way, place, lead] = state[lead] - lowest
            return state, lowest

        state, lowest = lax.fori_loop(
            0, tile_cols, body, (state, jnp.zeros(vreg, jnp.float32)), unroll=2
        )
        packed = state[0] - lowest
        for lead in range(1, LEADS):
            moved = pltpu.roll(state[lead] - lowest, lead, 1)
            packed = jnp.where(lane % span == lead, moved, packed)
        h_send[way] = packed

    def column_sweep(way, backward):
        state = tuple(v_recv[way, lead] for lead in range(LEADS))

        def body(index, state):
            place = jnp.where(backward, tile_rows - 1 - index, index)
            here = [v_cost[place, lead] for lead in range(LEADS)]
            state, lowest = advance(state, here)
            for lead in range(LEADS):
                v_path[way, place, lead] = state[lead] - lowest
            return tuple(value - lowest for value in state)

        state = lax.fori_loop(0, tile_rows, body, state)
        for lead in range(LEADS):
            v_send[way, lead] = state[lead]

    def horizontal(turn):
        right_half = col > cols - 1 - col
        backward = right_half if turn == 0 else jnp.logical_not(right_half)
        return run(
            "col", col, cols, backward, h_send, h_recv, h_send_sem, h_recv_sem, row_sweep
        )

    def vertical():
        def place_row(y, carried):
            block = ordered(volume_ref[y])
            for lead in range(LEADS):
                v_cost[y, lead] = block[lead * SUBS : lead * SUBS + SUBS]
            return carried

        lax.fori_loop(0, tile_rows, place_row, 0)

        def one(turn, carried):
            lower_half = row > rows - 1 - row
            backward = lower_half != (turn == 1)
            copy, sent = run(
                "row", row, rows, backward, v_send, v_recv, v_send_sem, v_recv_sem, column_sweep
            )

            @pl.when(sent)
            def _():
                copy.wait_send()

            return carried

        lax.fori_loop(0, 2, one, 0)

        def gather_row(y, carried):
            block = jnp.concatenate(
                [v_path[0, y, lead] + v_path[1, y, lead] for lead in range(LEADS)], axis=0
            )
            total[y] = restored(block)
            return carried

        lax.fori_loop(0, tile_rows, gather_row, 0)

    late = 2 * jnp.minimum(col, cols - 1 - col) >= cols // 2

    @pl.when(late)
    def _():
        vertical()

    first, first_sent = horizontal(0)

    @pl.when(jnp.logical_not(late))
    def _():
        vertical()

    second, second_sent = horizontal(1)

    def gather(group, carried):
        start = pl.multiple_of(group * span, span)
        pieces = []
        for lead in range(LEADS):
            merged = h_path[0, start, lead] + h_path[1, start, lead]
            for x in range(1, span):
                moved = pltpu.roll(h_path[0, start + x, lead] + h_path[1, start + x, lead], x, 1)
                merged = jnp.where(lane % span == x, moved, merged)
            pieces.append(merged)
        block = restored(jnp.concatenate(pieces, axis=0))
        for y in range(tile_rows):
            where = pl.ds(start, span)
            out_ref[y, where, :] = (
                (total[y, where, :] + block[y * span : y * span + span]) * 0.25
            ).astype(jnp.bfloat16)
        return carried

    lax.fori_loop(0, groups, gather, 0)

    @pl.when(first_sent)
    def _():
        first.wait_send()

    @pl.when(second_sent)
    def _():
        second.wait_send()


def aggregate(volume):
    tile_rows, tile_cols, disps = volume.shape
    vregs = (LEADS, SUBS, NDISP)
    return pl.pallas_call(
        partial(path_kernel, tile_rows, tile_cols),
        out_shape=jax.ShapeDtypeStruct(volume.shape, jnp.bfloat16),
        in_specs=[pl.BlockSpec(memory_space=pltpu.VMEM)],
        out_specs=pl.BlockSpec(memory_space=pltpu.VMEM),
        scratch_shapes=[
            pltpu.VMEM((tile_rows, *vregs), jnp.float32),
            pltpu.VMEM((tile_cols, *vregs), jnp.float32),
            pltpu.VMEM((2, tile_cols, *vregs), jnp.float32),
            pltpu.VMEM((2, tile_rows, *vregs), jnp.float32),
            pltpu.VMEM(volume.shape, jnp.float32),
            pltpu.VMEM((2, SUBS, NDISP), jnp.float32),
            pltpu.VMEM((2, SUBS, NDISP), jnp.float32),
            pltpu.VMEM((2, *vregs), jnp.float32),
            pltpu.VMEM((2, *vregs), jnp.float32),
            pltpu.SemaphoreType.DMA((2,)),
            pltpu.SemaphoreType.DMA((2,)),
            pltpu.SemaphoreType.DMA((2,)),
            pltpu.SemaphoreType.DMA((2,)),
        ],
        compiler_params=pltpu.CompilerParams(
            collective_id=0, has_side_effects=True, vmem_limit_bytes=48 << 20
        ),
        name="paths",
    )(volume)


def on_device(
    left_image, right_image, first_weight, second_weight, third_weight, tile_base, tile_width
):
    weights = (first_weight, second_weight, third_weight)
    tile_rows, tile_cols = left_image.shape
    rows, cols = lax.axis_size("row"), lax.axis_size("col")
    blocks = exchange(jnp.stack([left_image, right_image]).astype(jnp.float32))
    place = jnp.stack(
        [
            tile_base[0, 0],
            tile_width[0, 0],
            lax.axis_index("row") * tile_rows,
            lax.axis_index("col") * tile_cols,
            jnp.int32(rows * tile_rows),
            jnp.int32(cols * tile_cols),
        ]
    )
    return aggregate(cost_volume(place, blocks, weights))


def solution(mesh):
    placed = (P("row", "col"), P("row", "col"), P(), P(), P(), P("row", "col"), P("row", "col"))
    return jax.shard_map(
        on_device, mesh=mesh, in_specs=placed, out_specs=P("row", "col", None), check_vma=False
    )
```

```python
from functools import partial

import jax
import jax.numpy as jnp
from jax import lax
from jax.experimental import pallas as pl
from jax.experimental.pallas import tpu as pltpu
from jax.sharding import PartitionSpec as P

NDISP = 128
MESH = pl.DeviceIdType.MESH


PENALTY_SMALL = 0.5
PENALTY_LARGE = 4.0
INVALID_COST = 2.0
BIG_VALUE = 1e30


ROW_BLOCKS = 3
COL_BLOCKS = 4


def exchange_kernel(left_ref, right_ref, out_ref, own_ref, send_sem, recv_sem):
    cols, rows = lax.axis_size("col"), lax.axis_size("row")
    col, row = lax.axis_index("col"), lax.axis_index("row")
    barrier = pltpu.get_barrier_semaphore()
    moves = [
        (down, right)
        for down in (-1, 0, 1)
        for right in (-1, 0, 1, 2)
        if (down, right) != (0, 0)
    ]

    def exists(down, right):
        return (
            (row + down >= 0) & (row + down < rows) & (col + right >= 0) & (col + right < cols)
        )

    count = jnp.int32(0)
    for down, right in moves:

        @pl.when(exists(-down, -right))
        def _():
            pl.semaphore_signal(
                barrier,
                inc=1,
                device_id={"row": row - down, "col": col - right},
                device_id_type=MESH,
            )

        count = count + exists(down, right).astype(jnp.int32)
    for num, image in enumerate((left_ref, right_ref)):
        value = image[...].astype(jnp.float32)
        own_ref[num] = value
        out_ref[1, 2, num] = value
    pl.semaphore_wait(barrier, count)

    def copy_of(down, right):
        return pltpu.make_async_remote_copy(
            src_ref=own_ref,
            dst_ref=out_ref.at[1 - down, 2 - right],
            send_sem=send_sem.at[1 - down, 2 - right],
            recv_sem=recv_sem.at[1 - down, 2 - right],
            device_id={"row": row + down, "col": col + right},
            device_id_type=MESH,
        )

    for down, right in moves:

        @pl.when(exists(down, right))
        def _():
            copy_of(down, right).start()

        @pl.when(jnp.logical_not(exists(-down, -right)))
        def _():
            out_ref[1 - down, 2 - right] = jnp.zeros(own_ref.shape, jnp.float32)

    for down, right in moves:

        @pl.when(exists(-down, -right))
        def _():
            copy_of(down, right).wait_recv()

        @pl.when(exists(down, right))
        def _():
            copy_of(down, right).wait_send()


def exchange(left_image, right_image):
    pair = (2, *left_image.shape)
    return pl.pallas_call(
        exchange_kernel,
        out_shape=jax.ShapeDtypeStruct((ROW_BLOCKS, COL_BLOCKS, *pair), jnp.float32),
        in_specs=[pl.BlockSpec(memory_space=pltpu.VMEM)] * 2,
        out_specs=pl.BlockSpec(memory_space=pltpu.VMEM),
        scratch_shapes=[
            pltpu.VMEM(pair, jnp.float32),
            pltpu.SemaphoreType.DMA((ROW_BLOCKS, COL_BLOCKS)),
            pltpu.SemaphoreType.DMA((ROW_BLOCKS, COL_BLOCKS)),
        ],
        compiler_params=pltpu.CompilerParams(collective_id=1, has_side_effects=True),
        name="exchange",
    )(left_image, right_image)


def layer(source, weight, span, out_rows, rectify, inside):
    chans, length = source.shape
    stacked = jnp.concatenate(
        [pltpu.roll(source, 1, 1), source, pltpu.roll(source, length - 1, 1)], axis=0
    ).astype(jnp.bfloat16)
    result = jnp.zeros((weight.shape[0], out_rows * span), jnp.float32)
    for row_off in range(3):
        result = result + jnp.dot(
            weight[:, row_off * 3 * chans : (row_off + 1) * 3 * chans],
            stacked[:, row_off * span : (row_off + out_rows) * span],
            preferred_element_type=jnp.float32,
        )
    if rectify:
        result = jnp.maximum(result, 0.0)
    return jnp.where(inside, result, 0.0).astype(jnp.bfloat16).astype(jnp.float32)


def cost_kernel(
    tile_rows, tile_cols, place_ref, blocks_ref, first_ref, second_ref, third_ref, out_ref
):
    base, width = place_ref[0], place_ref[1]
    first_row, first_col = place_ref[2], place_ref[3]
    total_rows, total_cols = place_ref[4], place_ref[5]
    weights = (first_ref[...], second_ref[...], third_ref[...])

    def tower(image, blocks):
        span = len(blocks) * tile_cols
        lines = [
            jnp.concatenate([blocks_ref[0, j, image] for j in blocks], axis=1)[
                tile_rows - 3 : tile_rows
            ],
            jnp.concatenate([blocks_ref[1, j, image] for j in blocks], axis=1),
            jnp.concatenate([blocks_ref[2, j, image] for j in blocks], axis=1)[0:3],
        ]
        current = jnp.concatenate(
            [line[i : i + 1] for line in lines for i in range(line.shape[0])], axis=1
        )
        for num in range(3):
            out_rows = tile_rows + 4 - 2 * num
            index = lax.broadcasted_iota(jnp.int32, (1, out_rows * span), 1)
            row_place = first_row - 2 + num + index // span
            col_place = first_col + (blocks[0] - 2) * tile_cols + index % span
            inside = (
                (row_place >= 0)
                & (row_place < total_rows)
                & (col_place >= 0)
                & (col_place < total_cols)
            )
            current = layer(current, weights[num], span, out_rows, num < 2, inside)
        return current, span

    left, left_span = tower(0, (1, 2, 3))
    right, right_span = tower(1, (0, 1, 2, 3))
    ext = 2 * tile_cols
    flip = lax.broadcasted_iota(jnp.int32, (ext, ext), 0) + lax.broadcasted_iota(
        jnp.int32, (ext, ext), 1
    )
    flip = (flip == ext - 1).astype(jnp.float32).astype(jnp.bfloat16)
    shifts = lax.broadcasted_iota(jnp.int32, (tile_cols, NDISP), 1)
    in_range = (shifts >= base) & (shifts < base + width)
    for y in range(tile_rows):
        own = left[:, y * left_span + tile_cols : y * left_span + 2 * tile_cols].T
        other = right[:, y * right_span + tile_cols : y * right_span + 3 * tile_cols]
        other = jnp.dot(other.astype(jnp.bfloat16), flip, preferred_element_type=jnp.float32)
        own_norm = jnp.maximum(jnp.sqrt(jnp.sum(own * own, axis=1, keepdims=True)), 1.0)
        other_norm = jnp.maximum(jnp.sqrt(jnp.sum(other * other, axis=0, keepdims=True)), 1.0)
        products = jnp.dot(
            own.astype(jnp.bfloat16),
            other.astype(jnp.bfloat16),
            preferred_element_type=jnp.float32,
        )
        cosine = products / (own_norm * other_norm)
        cosine = pltpu.roll(cosine, ext - tile_cols + 1, 1, stride=1, stride_axis=0)
        out_ref[y] = jnp.where(in_range, 1.0 - cosine[:, :NDISP], INVALID_COST).astype(
            jnp.bfloat16
        )


def cost_volume(place, blocks, weights):
    tile_rows, tile_cols = blocks.shape[3:]
    return pl.pallas_call(
        partial(cost_kernel, tile_rows, tile_cols),
        out_shape=jax.ShapeDtypeStruct((tile_rows, tile_cols, NDISP), jnp.bfloat16),
        in_specs=[pl.BlockSpec(memory_space=pltpu.SMEM)]
        + [pl.BlockSpec(memory_space=pltpu.VMEM)] * 4,
        out_specs=pl.BlockSpec(memory_space=pltpu.VMEM),
        compiler_params=pltpu.CompilerParams(vmem_limit_bytes=32 << 20),
        name="costs",
    )(place, blocks, *weights)


def mesh_barrier(col, cols, row, rows):
    barrier = pltpu.get_barrier_semaphore()
    count = jnp.int32(0)
    for axis, place, size in (("col", col, cols), ("row", row, rows)):
        for step in (-1, 1):
            there = (place + step >= 0) & (place + step < size)

            @pl.when(there)
            def _():
                pl.semaphore_signal(
                    barrier, inc=1, device_id={axis: place + step}, device_id_type=MESH
                )

            count = count + there.astype(jnp.int32)
    return barrier, count


SUBS = 8
LEADS = NDISP // SUBS


def path_kernel(
    tile_rows,
    tile_cols,
    volume_ref,
    out_ref,
    v_cost,
    h_cost,
    h_path,
    v_path,
    total,
    h_send,
    h_recv,
    v_send,
    v_recv,
    h_send_sem,
    h_recv_sem,
    v_send_sem,
    v_recv_sem,
):
    cols, rows = lax.axis_size("col"), lax.axis_size("row")
    col, row = lax.axis_index("col"), lax.axis_index("row")
    barrier, count = mesh_barrier(col, cols, row, rows)
    span = NDISP // tile_rows
    groups = tile_cols // span
    vreg = (SUBS, NDISP)
    sub = lax.broadcasted_iota(jnp.int32, vreg, 0)
    lane = lax.broadcasted_iota(jnp.int32, vreg, 1)
    first_edge = jnp.where(sub == 0, BIG_VALUE, PENALTY_SMALL)
    last_edge = jnp.where(sub == SUBS - 1, BIG_VALUE, PENALTY_SMALL)
    near_row = lax.broadcasted_iota(jnp.int32, (NDISP, NDISP), 0)
    near_col = lax.broadcasted_iota(jnp.int32, (NDISP, NDISP), 1)
    order = ((near_row % SUBS) * LEADS + near_row // SUBS == near_col).astype(jnp.float32)
    order = order.astype(jnp.bfloat16)

    def ordered(block):
        return lax.dot_general(
            order, block, (((1,), (1,)), ((), ())), preferred_element_type=jnp.float32
        )

    def restored(block):
        turned = block.T
        high = turned.astype(jnp.bfloat16)
        low = (turned - high.astype(jnp.float32)).astype(jnp.bfloat16)
        return jnp.dot(high, order, preferred_element_type=jnp.float32) + jnp.dot(
            low, order, preferred_element_type=jnp.float32
        )

    def spread(group, carried):
        start = pl.multiple_of(group * span, span)
        block = jnp.concatenate(
            [volume_ref[y, pl.ds(start, span), :] for y in range(tile_rows)], axis=0
        )
        block = ordered(block)
        for lead in range(LEADS):
            piece = block[lead * SUBS : lead * SUBS + SUBS]
            for x in range(span):
                h_cost[start + x, lead] = pltpu.roll(piece, (NDISP - x) % NDISP, 1)
        return carried

    lax.fori_loop(0, groups, spread, 0)
    pl.semaphore_wait(barrier, count)

    def advance(state, here):
        lowest = list(state)
        while len(lowest) > 1:
            lowest = [jnp.minimum(lowest[i], lowest[i + 1]) for i in range(0, len(lowest), 2)]
        lowest = lowest[0]
        lowest = jnp.minimum(lowest, pltpu.roll(lowest, 4, 0))
        turned = [pltpu.roll(lowest, shift, 0) for shift in (1, 2, 3)]
        lowest = jnp.minimum(
            jnp.minimum(lowest, turned[0]), jnp.minimum(turned[1], turned[2])
        )
        jump = lowest + PENALTY_LARGE
        below = pltpu.roll(state[LEADS - 1], 1, 0) + first_edge
        above = pltpu.roll(state[0], SUBS - 1, 0) + last_edge
        ext = [below, *(value + PENALTY_SMALL for value in state), above]
        new = []
        for lead in range(LEADS):
            near = jnp.minimum(state[lead], jnp.minimum(ext[lead], ext[lead + 2]))
            new.append(jnp.minimum(near, jump) + here[lead])
        return tuple(new), lowest

    def run(axis, place, size, backward, send, recv, send_sem, recv_sem, sweep):
        way = backward.astype(jnp.int32)
        step = 1 - 2 * way
        has_source = (place - step >= 0) & (place - step < size)
        has_target = (place + step >= 0) & (place + step < size)
        copy = pltpu.make_async_remote_copy(
            src_ref=send.at[way],
            dst_ref=recv.at[way],
            send_sem=send_sem.at[way],
            recv_sem=recv_sem.at[way],
            device_id={axis: place + step},
            device_id_type=MESH,
        )

        @pl.when(has_source)
        def _():
            copy.wait_recv()

        @pl.when(jnp.logical_not(has_source))
        def _():
            recv[way] = jnp.zeros(recv.shape[1:], jnp.float32)

        sweep(way, backward)

        @pl.when(has_target)
        def _():
            copy.start()

        return copy, has_target

    def row_sweep(way, backward):
        packed = h_recv[way]
        state = tuple(pltpu.roll(packed, (NDISP - i) % NDISP, 1) for i in range(LEADS))

        def body(index, carried):
            place = jnp.where(backward, tile_cols - 1 - index, index)
            here = [h_cost[place, lead] for lead in range(LEADS)]
            state, lowest = advance(carried[0], here)
            for lead in range(LEADS):
                h_path[way, place, lead] = state[lead] - lowest
            return state, lowest

        state, lowest = lax.fori_loop(
            0, tile_cols, body, (state, jnp.zeros(vreg, jnp.float32)), unroll=8
        )
        packed = state[0] - lowest
        for lead in range(1, LEADS):
            moved = pltpu.roll(state[lead] - lowest, lead, 1)
            packed = jnp.where(lane % span == lead, moved, packed)
        h_send[way] = packed

    def column_sweep(way, backward):
        state = tuple(v_recv[way, lead] for lead in range(LEADS))

        def body(index, state):
            place = jnp.where(backward, tile_rows - 1 - index, index)
            here = [v_cost[place, lead] for lead in range(LEADS)]
            state, lowest = advance(state, here)
            for lead in range(LEADS):
                v_path[way, place, lead] = state[lead] - lowest
            return tuple(value - lowest for value in state)

        state = lax.fori_loop(0, tile_rows, body, state)
        for lead in range(LEADS):
            v_send[way, lead] = state[lead]

    def horizontal(turn):
        right_half = col > cols - 1 - col
        backward = right_half if turn == 0 else jnp.logical_not(right_half)
        return run(
            "col", col, cols, backward, h_send, h_recv, h_send_sem, h_recv_sem, row_sweep
        )

    def vertical():
        def place_row(y, carried):
            block = ordered(volume_ref[y])
            for lead in range(LEADS):
                v_cost[y, lead] = block[lead * SUBS : lead * SUBS + SUBS]
            return carried

        lax.fori_loop(0, tile_rows, place_row, 0)

        def one(turn, carried):
            lower_half = row > rows - 1 - row
            backward = lower_half != (turn == 1)
            copy, sent = run(
                "row", row, rows, backward, v_send, v_recv, v_send_sem, v_recv_sem, column_sweep
            )

            @pl.when(sent)
            def _():
                copy.wait_send()

            return carried

        lax.fori_loop(0, 2, one, 0)

        def gather_row(y, carried):
            block = jnp.concatenate(
                [v_path[0, y, lead] + v_path[1, y, lead] for lead in range(LEADS)], axis=0
            )
            total[y] = restored(block)
            return carried

        lax.fori_loop(0, tile_rows, gather_row, 0)

    late = 2 * jnp.minimum(col, cols - 1 - col) >= cols // 2

    @pl.when(late)
    def _():
        vertical()

    first, first_sent = horizontal(0)

    @pl.when(jnp.logical_not(late))
    def _():
        vertical()

    second, second_sent = horizontal(1)

    def gather(group, carried):
        start = pl.multiple_of(group * span, span)
        pieces = []
        for lead in range(LEADS):
            merged = h_path[0, start, lead] + h_path[1, start, lead]
            for x in range(1, span):
                moved = pltpu.roll(h_path[0, start + x, lead] + h_path[1, start + x, lead], x, 1)
                merged = jnp.where(lane % span == x, moved, merged)
            pieces.append(merged)
        block = restored(jnp.concatenate(pieces, axis=0))
        for y in range(tile_rows):
            where = pl.ds(start, span)
            out_ref[y, where, :] = (
                (total[y, where, :] + block[y * span : y * span + span]) * 0.25
            ).astype(jnp.bfloat16)
        return carried

    lax.fori_loop(0, groups, gather, 0)

    @pl.when(first_sent)
    def _():
        first.wait_send()

    @pl.when(second_sent)
    def _():
        second.wait_send()


def aggregate(volume):
    tile_rows, tile_cols, disps = volume.shape
    vregs = (LEADS, SUBS, NDISP)
    return pl.pallas_call(
        partial(path_kernel, tile_rows, tile_cols),
        out_shape=jax.ShapeDtypeStruct(volume.shape, jnp.bfloat16),
        in_specs=[pl.BlockSpec(memory_space=pltpu.VMEM)],
        out_specs=pl.BlockSpec(memory_space=pltpu.VMEM),
        scratch_shapes=[
            pltpu.VMEM((tile_rows, *vregs), jnp.float32),
            pltpu.VMEM((tile_cols, *vregs), jnp.float32),
            pltpu.VMEM((2, tile_cols, *vregs), jnp.float32),
            pltpu.VMEM((2, tile_rows, *vregs), jnp.float32),
            pltpu.VMEM(volume.shape, jnp.float32),
            pltpu.VMEM((2, SUBS, NDISP), jnp.float32),
            pltpu.VMEM((2, SUBS, NDISP), jnp.float32),
            pltpu.VMEM((2, *vregs), jnp.float32),
            pltpu.VMEM((2, *vregs), jnp.float32),
            pltpu.SemaphoreType.DMA((2,)),
            pltpu.SemaphoreType.DMA((2,)),
            pltpu.SemaphoreType.DMA((2,)),
            pltpu.SemaphoreType.DMA((2,)),
        ],
        compiler_params=pltpu.CompilerParams(
            collective_id=0, has_side_effects=True, vmem_limit_bytes=48 << 20
        ),
        name="paths",
    )(volume)


def on_device(
    left_image, right_image, first_weight, second_weight, third_weight, tile_base, tile_width
):
    weights = (first_weight, second_weight, third_weight)
    tile_rows, tile_cols = left_image.shape
    rows, cols = lax.axis_size("row"), lax.axis_size("col")
    blocks = exchange(left_image, right_image)
    place = jnp.stack(
        [
            tile_base[0, 0],
            tile_width[0, 0],
            lax.axis_index("row") * tile_rows,
            lax.axis_index("col") * tile_cols,
            jnp.int32(rows * tile_rows),
            jnp.int32(cols * tile_cols),
        ]
    )
    return aggregate(cost_volume(place, blocks, weights))


def solution(mesh):
    placed = (P("row", "col"), P("row", "col"), P(), P(), P(), P("row", "col"), P("row", "col"))
    return jax.shard_map(
        on_device, mesh=mesh, in_specs=placed, out_specs=P("row", "col", None), check_vma=False
    )
```

```python
from functools import partial

import jax
import jax.numpy as jnp
from jax import lax
from jax.experimental import pallas as pl
from jax.experimental.pallas import tpu as pltpu
from jax.sharding import PartitionSpec as P

NDISP = 128
MESH = pl.DeviceIdType.MESH


PENALTY_SMALL = 0.5
PENALTY_LARGE = 4.0
INVALID_COST = 2.0
BIG_VALUE = 1e30


ROW_BLOCKS = 3
COL_BLOCKS = 4


def exchange_kernel(left_ref, right_ref, out_ref, own_ref, send_sem, recv_sem):
    cols, rows = lax.axis_size("col"), lax.axis_size("row")
    col, row = lax.axis_index("col"), lax.axis_index("row")
    barrier = pltpu.get_barrier_semaphore()
    moves = [
        (down, right)
        for down in (-1, 0, 1)
        for right in (-1, 0, 1, 2)
        if (down, right) != (0, 0)
    ]

    def exists(down, right):
        return (
            (row + down >= 0) & (row + down < rows) & (col + right >= 0) & (col + right < cols)
        )

    count = jnp.int32(0)
    for down, right in moves:

        @pl.when(exists(-down, -right))
        def _():
            pl.semaphore_signal(
                barrier,
                inc=1,
                device_id={"row": row - down, "col": col - right},
                device_id_type=MESH,
            )

        count = count + exists(down, right).astype(jnp.int32)
    for num, image in enumerate((left_ref, right_ref)):
        value = image[...].astype(jnp.float32)
        own_ref[num] = value
        out_ref[1, 2, num] = value
    pl.semaphore_wait(barrier, count)

    def copy_of(down, right):
        return pltpu.make_async_remote_copy(
            src_ref=own_ref,
            dst_ref=out_ref.at[1 - down, 2 - right],
            send_sem=send_sem.at[1 - down, 2 - right],
            recv_sem=recv_sem.at[1 - down, 2 - right],
            device_id={"row": row + down, "col": col + right},
            device_id_type=MESH,
        )

    for down, right in moves:

        @pl.when(exists(down, right))
        def _():
            copy_of(down, right).start()

        @pl.when(jnp.logical_not(exists(-down, -right)))
        def _():
            out_ref[1 - down, 2 - right] = jnp.zeros(own_ref.shape, jnp.float32)

    for down, right in moves:

        @pl.when(exists(-down, -right))
        def _():
            copy_of(down, right).wait_recv()

        @pl.when(exists(down, right))
        def _():
            copy_of(down, right).wait_send()


def exchange(left_image, right_image):
    pair = (2, *left_image.shape)
    return pl.pallas_call(
        exchange_kernel,
        out_shape=jax.ShapeDtypeStruct((ROW_BLOCKS, COL_BLOCKS, *pair), jnp.float32),
        in_specs=[pl.BlockSpec(memory_space=pltpu.VMEM)] * 2,
        out_specs=pl.BlockSpec(memory_space=pltpu.VMEM),
        scratch_shapes=[
            pltpu.VMEM(pair, jnp.float32),
            pltpu.SemaphoreType.DMA((ROW_BLOCKS, COL_BLOCKS)),
            pltpu.SemaphoreType.DMA((ROW_BLOCKS, COL_BLOCKS)),
        ],
        compiler_params=pltpu.CompilerParams(collective_id=1, has_side_effects=True),
        name="exchange",
    )(left_image, right_image)


def layer(source, weight, span, out_rows, rectify, inside):
    chans, length = source.shape
    stacked = jnp.concatenate(
        [pltpu.roll(source, 1, 1), source, pltpu.roll(source, length - 1, 1)], axis=0
    ).astype(jnp.bfloat16)
    result = jnp.zeros((weight.shape[0], out_rows * span), jnp.float32)
    for row_off in range(3):
        result = result + jnp.dot(
            weight[:, row_off * 3 * chans : (row_off + 1) * 3 * chans],
            stacked[:, row_off * span : (row_off + out_rows) * span],
            preferred_element_type=jnp.float32,
        )
    if rectify:
        result = jnp.maximum(result, 0.0)
    return jnp.where(inside, result, 0.0).astype(jnp.bfloat16).astype(jnp.float32)


def cost_kernel(
    tile_rows, tile_cols, place_ref, blocks_ref, first_ref, second_ref, third_ref, out_ref
):
    base, width = place_ref[0], place_ref[1]
    first_row, first_col = place_ref[2], place_ref[3]
    total_rows, total_cols = place_ref[4], place_ref[5]
    weights = (first_ref[...], second_ref[...], third_ref[...])

    def tower(image, blocks):
        span = len(blocks) * tile_cols
        lines = [
            jnp.concatenate([blocks_ref[0, j, image] for j in blocks], axis=1)[
                tile_rows - 3 : tile_rows
            ],
            jnp.concatenate([blocks_ref[1, j, image] for j in blocks], axis=1),
            jnp.concatenate([blocks_ref[2, j, image] for j in blocks], axis=1)[0:3],
        ]
        current = jnp.concatenate(
            [line[i : i + 1] for line in lines for i in range(line.shape[0])], axis=1
        )
        for num in range(3):
            out_rows = tile_rows + 4 - 2 * num
            index = lax.broadcasted_iota(jnp.int32, (1, out_rows * span), 1)
            row_place = first_row - 2 + num + index // span
            col_place = first_col + (blocks[0] - 2) * tile_cols + index % span
            inside = (
                (row_place >= 0)
                & (row_place < total_rows)
                & (col_place >= 0)
                & (col_place < total_cols)
            )
            current = layer(current, weights[num], span, out_rows, num < 2, inside)
        return current, span

    left, left_span = tower(0, (1, 2, 3))
    right, right_span = tower(1, (0, 1, 2, 3))
    ext = 2 * tile_cols
    flip = lax.broadcasted_iota(jnp.int32, (ext, ext), 0) + lax.broadcasted_iota(
        jnp.int32, (ext, ext), 1
    )
    flip = (flip == ext - 1).astype(jnp.float32).astype(jnp.bfloat16)
    shifts = lax.broadcasted_iota(jnp.int32, (tile_cols, NDISP), 1)
    in_range = (shifts >= base) & (shifts < base + width)
    for y in range(tile_rows):
        own = left[:, y * left_span + tile_cols : y * left_span + 2 * tile_cols].T
        other = right[:, y * right_span + tile_cols : y * right_span + 3 * tile_cols]
        other = jnp.dot(other.astype(jnp.bfloat16), flip, preferred_element_type=jnp.float32)
        own_norm = jnp.maximum(jnp.sqrt(jnp.sum(own * own, axis=1, keepdims=True)), 1.0)
        other_norm = jnp.maximum(jnp.sqrt(jnp.sum(other * other, axis=0, keepdims=True)), 1.0)
        products = jnp.dot(
            own.astype(jnp.bfloat16),
            other.astype(jnp.bfloat16),
            preferred_element_type=jnp.float32,
        )
        cosine = products / (own_norm * other_norm)
        cosine = pltpu.roll(cosine, ext - tile_cols + 1, 1, stride=1, stride_axis=0)
        out_ref[y] = jnp.where(in_range, 1.0 - cosine[:, :NDISP], INVALID_COST).astype(
            jnp.bfloat16
        )


def cost_volume(place, blocks, weights):
    tile_rows, tile_cols = blocks.shape[3:]
    return pl.pallas_call(
        partial(cost_kernel, tile_rows, tile_cols),
        out_shape=jax.ShapeDtypeStruct((tile_rows, tile_cols, NDISP), jnp.bfloat16),
        in_specs=[pl.BlockSpec(memory_space=pltpu.SMEM)]
        + [pl.BlockSpec(memory_space=pltpu.VMEM)] * 4,
        out_specs=pl.BlockSpec(memory_space=pltpu.VMEM),
        compiler_params=pltpu.CompilerParams(vmem_limit_bytes=32 << 20),
        name="costs",
    )(place, blocks, *weights)


def mesh_barrier(col, cols, row, rows):
    barrier = pltpu.get_barrier_semaphore()
    count = jnp.int32(0)
    for axis, place, size in (("col", col, cols), ("row", row, rows)):
        for step in (-1, 1):
            there = (place + step >= 0) & (place + step < size)

            @pl.when(there)
            def _():
                pl.semaphore_signal(
                    barrier, inc=1, device_id={axis: place + step}, device_id_type=MESH
                )

            count = count + there.astype(jnp.int32)
    return barrier, count


SUBS = 8
LEADS = NDISP // SUBS


def path_kernel(
    tile_rows,
    tile_cols,
    volume_ref,
    out_ref,
    v_cost,
    h_cost,
    h_path,
    v_path,
    total,
    h_send,
    h_recv,
    v_send,
    v_recv,
    h_send_sem,
    h_recv_sem,
    v_send_sem,
    v_recv_sem,
):
    cols, rows = lax.axis_size("col"), lax.axis_size("row")
    col, row = lax.axis_index("col"), lax.axis_index("row")
    barrier, count = mesh_barrier(col, cols, row, rows)
    span = NDISP // tile_rows
    groups = tile_cols // span
    vreg = (SUBS, NDISP)
    sub = lax.broadcasted_iota(jnp.int32, vreg, 0)
    lane = lax.broadcasted_iota(jnp.int32, vreg, 1)
    first_edge = jnp.where(sub == 0, BIG_VALUE, PENALTY_SMALL)
    last_edge = jnp.where(sub == SUBS - 1, BIG_VALUE, PENALTY_SMALL)
    near_row = lax.broadcasted_iota(jnp.int32, (NDISP, NDISP), 0)
    near_col = lax.broadcasted_iota(jnp.int32, (NDISP, NDISP), 1)
    order = ((near_row % SUBS) * LEADS + near_row // SUBS == near_col).astype(jnp.float32)
    order = order.astype(jnp.bfloat16)

    def ordered(block):
        return lax.dot_general(
            order, block, (((1,), (1,)), ((), ())), preferred_element_type=jnp.float32
        )

    def restored(block):
        turned = block.T
        high = turned.astype(jnp.bfloat16)
        low = (turned - high.astype(jnp.float32)).astype(jnp.bfloat16)
        return jnp.dot(high, order, preferred_element_type=jnp.float32) + jnp.dot(
            low, order, preferred_element_type=jnp.float32
        )

    def spread(group, carried):
        start = pl.multiple_of(group * span, span)
        block = jnp.concatenate(
            [volume_ref[y, pl.ds(start, span), :] for y in range(tile_rows)], axis=0
        )
        block = ordered(block)
        for lead in range(LEADS):
            piece = block[lead * SUBS : lead * SUBS + SUBS]
            for x in range(span):
                h_cost[start + x, lead] = pltpu.roll(piece, (NDISP - x) % NDISP, 1)
        return carried

    lax.fori_loop(0, groups, spread, 0)
    pl.semaphore_wait(barrier, count)

    def advance(state, here):
        lowest = list(state)
        while len(lowest) > 1:
            lowest = [jnp.minimum(lowest[i], lowest[i + 1]) for i in range(0, len(lowest), 2)]
        lowest = lowest[0]
        lowest = jnp.minimum(lowest, pltpu.roll(lowest, 4, 0))
        turned = [pltpu.roll(lowest, shift, 0) for shift in (1, 2, 3)]
        lowest = jnp.minimum(
            jnp.minimum(lowest, turned[0]), jnp.minimum(turned[1], turned[2])
        )
        jump = lowest + PENALTY_LARGE
        below = pltpu.roll(state[LEADS - 1], 1, 0) + first_edge
        above = pltpu.roll(state[0], SUBS - 1, 0) + last_edge
        ext = [below, *(value + PENALTY_SMALL for value in state), above]
        new = []
        for lead in range(LEADS):
            near = jnp.minimum(state[lead], jnp.minimum(ext[lead], ext[lead + 2]))
            new.append(jnp.minimum(near, jump) + here[lead])
        return tuple(new), lowest

    def run(axis, place, size, backward, send, recv, send_sem, recv_sem, sweep):
        way = backward.astype(jnp.int32)
        step = 1 - 2 * way
        has_source = (place - step >= 0) & (place - step < size)
        has_target = (place + step >= 0) & (place + step < size)
        copy = pltpu.make_async_remote_copy(
            src_ref=send.at[way],
            dst_ref=recv.at[way],
            send_sem=send_sem.at[way],
            recv_sem=recv_sem.at[way],
            device_id={axis: place + step},
            device_id_type=MESH,
        )

        @pl.when(has_source)
        def _():
            copy.wait_recv()

        @pl.when(jnp.logical_not(has_source))
        def _():
            recv[way] = jnp.zeros(recv.shape[1:], jnp.float32)

        sweep(way, backward)

        @pl.when(has_target)
        def _():
            copy.start()

        return copy, has_target

    def row_sweep(way, backward):
        packed = h_recv[way]
        state = tuple(pltpu.roll(packed, (NDISP - i) % NDISP, 1) for i in range(LEADS))

        def body(index, carried):
            place = jnp.where(backward, tile_cols - 1 - index, index)
            here = [h_cost[place, lead] for lead in range(LEADS)]
            state, lowest = advance(carried[0], here)
            for lead in range(LEADS):
                h_path[way, place, lead] = state[lead] - lowest
            return state, lowest

        state, lowest = lax.fori_loop(
            0, tile_cols, body, (state, jnp.zeros(vreg, jnp.float32)), unroll=8
        )
        packed = state[0] - lowest
        for lead in range(1, LEADS):
            moved = pltpu.roll(state[lead] - lowest, lead, 1)
            packed = jnp.where(lane % span == lead, moved, packed)
        h_send[way] = packed

    def column_sweep(way, backward):
        state = tuple(v_recv[way, lead] for lead in range(LEADS))

        def body(index, state):
            place = jnp.where(backward, tile_rows - 1 - index, index)
            here = [v_cost[place, lead] for lead in range(LEADS)]
            state, lowest = advance(state, here)
            for lead in range(LEADS):
                v_path[way, place, lead] = state[lead] - lowest
            return tuple(value - lowest for value in state)

        state = lax.fori_loop(0, tile_rows, body, state)
        for lead in range(LEADS):
            v_send[way, lead] = state[lead]

    def horizontal(turn):
        right_half = col > cols - 1 - col
        backward = right_half if turn == 0 else jnp.logical_not(right_half)
        return run(
            "col", col, cols, backward, h_send, h_recv, h_send_sem, h_recv_sem, row_sweep
        )

    def vertical():
        def place_row(y, carried):
            block = ordered(volume_ref[y])
            for lead in range(LEADS):
                v_cost[y, lead] = block[lead * SUBS : lead * SUBS + SUBS]
            return carried

        lax.fori_loop(0, tile_rows, place_row, 0)

        def one(turn, carried):
            lower_half = row > rows - 1 - row
            backward = lower_half != (turn == 1)
            copy, sent = run(
                "row", row, rows, backward, v_send, v_recv, v_send_sem, v_recv_sem, column_sweep
            )

            @pl.when(sent)
            def _():
                copy.wait_send()

            return carried

        lax.fori_loop(0, 2, one, 0)

        def gather_row(y, carried):
            block = jnp.concatenate(
                [v_path[0, y, lead] + v_path[1, y, lead] for lead in range(LEADS)], axis=0
            )
            total[y] = restored(block)
            return carried

        lax.fori_loop(0, tile_rows, gather_row, 0)

    late = 2 * jnp.minimum(col, cols - 1 - col) > cols // 2

    @pl.when(late)
    def _():
        vertical()

    first, first_sent = horizontal(0)

    @pl.when(jnp.logical_not(late))
    def _():
        vertical()

    second, second_sent = horizontal(1)

    def gather(group, carried):
        start = pl.multiple_of(group * span, span)
        pieces = []
        for lead in range(LEADS):
            merged = h_path[0, start, lead] + h_path[1, start, lead]
            for x in range(1, span):
                moved = pltpu.roll(h_path[0, start + x, lead] + h_path[1, start + x, lead], x, 1)
                merged = jnp.where(lane % span == x, moved, merged)
            pieces.append(merged)
        block = restored(jnp.concatenate(pieces, axis=0))
        for y in range(tile_rows):
            where = pl.ds(start, span)
            out_ref[y, where, :] = (
                (total[y, where, :] + block[y * span : y * span + span]) * 0.25
            ).astype(jnp.bfloat16)
        return carried

    lax.fori_loop(0, groups, gather, 0)

    @pl.when(first_sent)
    def _():
        first.wait_send()

    @pl.when(second_sent)
    def _():
        second.wait_send()


def aggregate(volume):
    tile_rows, tile_cols, disps = volume.shape
    vregs = (LEADS, SUBS, NDISP)
    return pl.pallas_call(
        partial(path_kernel, tile_rows, tile_cols),
        out_shape=jax.ShapeDtypeStruct(volume.shape, jnp.bfloat16),
        in_specs=[pl.BlockSpec(memory_space=pltpu.VMEM)],
        out_specs=pl.BlockSpec(memory_space=pltpu.VMEM),
        scratch_shapes=[
            pltpu.VMEM((tile_rows, *vregs), jnp.float32),
            pltpu.VMEM((tile_cols, *vregs), jnp.float32),
            pltpu.VMEM((2, tile_cols, *vregs), jnp.float32),
            pltpu.VMEM((2, tile_rows, *vregs), jnp.float32),
            pltpu.VMEM(volume.shape, jnp.float32),
            pltpu.VMEM((2, SUBS, NDISP), jnp.float32),
            pltpu.VMEM((2, SUBS, NDISP), jnp.float32),
            pltpu.VMEM((2, *vregs), jnp.float32),
            pltpu.VMEM((2, *vregs), jnp.float32),
            pltpu.SemaphoreType.DMA((2,)),
            pltpu.SemaphoreType.DMA((2,)),
            pltpu.SemaphoreType.DMA((2,)),
            pltpu.SemaphoreType.DMA((2,)),
        ],
        compiler_params=pltpu.CompilerParams(
            collective_id=0, has_side_effects=True, vmem_limit_bytes=48 << 20
        ),
        name="paths",
    )(volume)


def on_device(
    left_image, right_image, first_weight, second_weight, third_weight, tile_base, tile_width
):
    weights = (first_weight, second_weight, third_weight)
    tile_rows, tile_cols = left_image.shape
    rows, cols = lax.axis_size("row"), lax.axis_size("col")
    blocks = exchange(left_image, right_image)
    place = jnp.stack(
        [
            tile_base[0, 0],
            tile_width[0, 0],
            lax.axis_index("row") * tile_rows,
            lax.axis_index("col") * tile_cols,
            jnp.int32(rows * tile_rows),
            jnp.int32(cols * tile_cols),
        ]
    )
    return aggregate(cost_volume(place, blocks, weights))


def solution(mesh):
    placed = (P("row", "col"), P("row", "col"), P(), P(), P(), P("row", "col"), P("row", "col"))
    return jax.shard_map(
        on_device, mesh=mesh, in_specs=placed, out_specs=P("row", "col", None), check_vma=False
    )
```
